32 devices in a mesh: lon: 8 (over z, y), lat: 4 (over x, core).
Axes of the slice: x: 2, y: 2, z: 4, core: 2. Of those that a mesh axis runs over, the one named last changes fastest.
Arguments:
- crosswise_speed_units: float32 [8, 64, 2048], P(None, 'lat', 'lon'), may hold values from -6 to 6
- poleward_speed_units: float32 [8, 64, 2048], P(None, 'lat', 'lon'), may hold values from -6 to 6
- thermal_anomaly: float32 [8, 64, 2048], P(None, 'lat', 'lon'), may hold values from -6 to 6
- saltiness_anomaly: float32 [8, 64, 2048], P(None, 'lat', 'lon'), may hold values from -6 to 6
- freeboard_elevation: float32 [64, 2048], P('lat', 'lon'), may hold values from -6 to 6
- barotropic_zonal_flow: float32 [64, 2048], P('lat', 'lon'), may hold values from -6 to 6
- barotropic_meridional_flow: float32 [64, 2048], P('lat', 'lon'), may hold values from -6 to 6
- submerged_layer_tally: int32 [64, 2048], P('lat', 'lon'), may hold values from 0 to 8
- seam_partner_index: int32 [2048], P('lon'), may hold values from 0 to 2047, as said below
Outputs:
- zonal_speed_final: float32 [8, 64, 2048], P(None, 'lat', 'lon')
- poleward_speed_final: float32 [8, 64, 2048], P(None, 'lat', 'lon')
- thermal_final: float32 [8, 64, 2048], P(None, 'lat', 'lon')
- saltiness_final: float32 [8, 64, 2048], P(None, 'lat', 'lon')
- freeboard_final: float32 [64, 2048], P('lat', 'lon')
- barotropic_zonal_final: float32 [64, 2048], P('lat', 'lon')
- barotropic_meridional_final: float32 [64, 2048], P('lat', 'lon')
The draws below stay inside these ranges and needn't reach their ends.
Inputs may be any that keep to these rules, and one draw needn't show every extreme that they name: seam_partner_index[seam_partner_index[c]] = c, and seam_partner_index[(c + 1) mod 2048] = (seam_partner_index[c] - 1) mod 2048 for every column c.
All inputs are finite; a program needn't handle non-finite values.
Results may differ from the reference program's by a relative error of at most 0.0003.
Values sent between devices are 32-bit elements; how exact they have to be, the bound alone decides.
No kernel may reach another device: no remote copies, remote signals or barrier semaphores. Data moves between devices by JAX's collectives and lax.ppermute only.
A program may use at most 128 MiB of HBM per device.

```python
import jax
import jax.numpy as jnp
from jax import lax

VERTICAL_LAYERS = 8
SUBSTEPS = 12
MESH_YCOUNT = 64
MESH_XCOUNT = 2048


def draw_seam_partner_index(key, part):
    offset = jax.random.randint(jax.random.fold_in(key, 7), (), 0, MESH_XCOUNT)
    return jnp.remainder(offset - jnp.arange(MESH_XCOUNT, dtype=jnp.int32), MESH_XCOUNT).astype(jnp.int32)


def draw_submerged_layer_tally(key, part):
    selector = jax.random.randint(jax.random.fold_in(key, 11), (MESH_YCOUNT, MESH_XCOUNT), 0, 4)
    shallow = jax.random.randint(jax.random.fold_in(key, 12), (MESH_YCOUNT, MESH_XCOUNT), 0, VERTICAL_LAYERS + 1)
    return jnp.where(selector == 0, shallow, VERTICAL_LAYERS).astype(jnp.int32)


def shard_levels(key, dims, cuts, least, high):
    factor_of, own = 1.0, jax.random.fold_in(key, 6)
    for dim, parts in cuts:
        steps = jnp.exp(jax.random.uniform(jax.random.fold_in(own, dim), (parts,), jnp.float32, least / len(cuts), high / len(cuts)))
        factor_of = factor_of * jnp.repeat(steps, dims[dim] // parts).reshape([-1 if axis == dim else 1 for axis in range(len(dims))])
    return factor_of


def normal_values(own_key, shape, scale, bound, cuts=(), kind=jnp.bfloat16):
    gain = shard_levels(own_key, shape, cuts, -0.22, 0.18) if cuts else 1.0
    values = jax.random.normal(own_key, shape, jnp.float32) * scale * gain
    return jnp.minimum(jnp.maximum(values, -bound), bound).astype(kind)


def setup_inputs(seed: int = 0) -> dict:
    key_of = jax.random.split(jax.random.key(seed), 10)
    return {
        "crosswise_speed_units": normal_values(key_of[0], (VERTICAL_LAYERS, MESH_YCOUNT, MESH_XCOUNT), 1.0, 6.0, ((1, 4), (2, 8)), jnp.float32),
        "poleward_speed_units": normal_values(key_of[1], (VERTICAL_LAYERS, MESH_YCOUNT, MESH_XCOUNT), 1.0, 6.0, ((1, 4), (2, 8)), jnp.float32),
        "thermal_anomaly": normal_values(key_of[2], (VERTICAL_LAYERS, MESH_YCOUNT, MESH_XCOUNT), 1.0, 6.0, ((1, 4), (2, 8)), jnp.float32),
        "saltiness_anomaly": normal_values(key_of[3], (VERTICAL_LAYERS, MESH_YCOUNT, MESH_XCOUNT), 1.0, 6.0, ((1, 4), (2, 8)), jnp.float32),
        "freeboard_elevation": normal_values(key_of[4], (MESH_YCOUNT, MESH_XCOUNT), 1.0, 6.0, ((0, 4), (1, 8)), jnp.float32),
        "barotropic_zonal_flow": normal_values(key_of[5], (MESH_YCOUNT, MESH_XCOUNT), 1.0, 6.0, ((0, 4), (1, 8)), jnp.float32),
        "barotropic_meridional_flow": normal_values(key_of[6], (MESH_YCOUNT, MESH_XCOUNT), 1.0, 6.0, ((0, 4), (1, 8)), jnp.float32),
        "submerged_layer_tally": draw_submerged_layer_tally(jax.random.fold_in(key_of[9], 71), 0),
        "seam_partner_index": draw_seam_partner_index(jax.random.fold_in(key_of[9], 71), 0),
    }


COURANT = 0.15
PRESSURE_GAIN = 0.1
CORIOLIS = 0.3
WAVE_MASS = 1.2
WAVE_MOMENTUM = 1.2
EPSILON = 1e-6


def weno_face(far_up, near_up, centre, near_down, far_down):
    poly_zero = (2.0 * far_up - 7.0 * near_up + 11.0 * centre) / 6.0
    poly_one = (-near_up + 5.0 * centre + 2.0 * near_down) / 6.0
    poly_two = (2.0 * centre + 5.0 * near_down - far_down) / 6.0
    smooth_zero = 13.0 / 12.0 * (far_up - 2.0 * near_up + centre) ** 2 + 0.25 * (far_up - 4.0 * near_up + 3.0 * centre) ** 2
    smooth_one = 13.0 / 12.0 * (near_up - 2.0 * centre + near_down) ** 2 + 0.25 * (near_up - near_down) ** 2
    smooth_two = 13.0 / 12.0 * (centre - 2.0 * near_down + far_down) ** 2 + 0.25 * (3.0 * centre - 4.0 * near_down + far_down) ** 2
    weight_zero = 0.1 / (EPSILON + smooth_zero) ** 2
    weight_one = 0.6 / (EPSILON + smooth_one) ** 2
    weight_two = 0.3 / (EPSILON + smooth_two) ** 2
    return (weight_zero * poly_zero + weight_one * poly_one + weight_two * poly_two) / (weight_zero + weight_one + weight_two)


def face_fluxes(prognostic_bundle, velocity, wet_mask, along, length):
    def window(values, offset):
        return lax.slice_in_dim(values, offset, offset + length + 1, axis=along)

    face_speed = 0.5 * (window(velocity, 2) + window(velocity, 3)) * window(wet_mask, 2) * window(wet_mask, 3)
    upwind = weno_face(window(prognostic_bundle, 0), window(prognostic_bundle, 1), window(prognostic_bundle, 2), window(prognostic_bundle, 3), window(prognostic_bundle, 4))
    downwind = weno_face(window(prognostic_bundle, 5), window(prognostic_bundle, 4), window(prognostic_bundle, 3), window(prognostic_bundle, 2), window(prognostic_bundle, 1))
    fluxes = COURANT * face_speed * jnp.where(face_speed >= 0.0, upwind, downwind)
    return fluxes, face_speed


def wrap_columns(values, margin):
    return jnp.concatenate([values[..., -margin:], values, values[..., :margin]], axis=-1)


def fold_rows(values, margin, parity, seam_partner_index):
    southern = jnp.zeros(values.shape[:-2] + (margin, values.shape[-1]), jnp.float32)
    northern = parity * jnp.take(jnp.flip(values[..., -margin:, :], axis=-2), seam_partner_index, axis=-1)
    return jnp.concatenate([southern, values, northern], axis=-2)


def reference(crosswise_speed_units, poleward_speed_units, thermal_anomaly, saltiness_anomaly, freeboard_elevation, barotropic_zonal_flow, barotropic_meridional_flow, submerged_layer_tally, seam_partner_index):
    levels, lat_count, lon_count = crosswise_speed_units.shape
    level_index = lax.broadcasted_iota(jnp.int32, (levels, 1, 1), 0)
    submerged_indicator = (level_index < submerged_layer_tally[None]).astype(jnp.float32)
    wet_column = (submerged_layer_tally > 0).astype(jnp.float32)
    row_index = lax.broadcasted_iota(jnp.int32, (lat_count, 1), 0).astype(jnp.float32)
    coriolis = CORIOLIS * (2.0 * (row_index + 0.5) / lat_count - 1.0)
    field_parity = jnp.array([-1.0, -1.0, 1.0, 1.0], jnp.float32)[:, None, None]
    seawater_buoyancy_mass = 0.8 * saltiness_anomaly - 0.2 * thermal_anomaly
    pressure = jnp.cumsum(seawater_buoyancy_mass, axis=0) - 0.5 * seawater_buoyancy_mass
    prognostic_bundle = jnp.stack([crosswise_speed_units, poleward_speed_units, thermal_anomaly, saltiness_anomaly], axis=1)

    def horizontal(inputs):
        level_fields, wet_mask, pressure_level = inputs
        east_west = wrap_columns(level_fields, 3)
        wet_east = wrap_columns(wet_mask, 3)
        flux_east, speed_east = face_fluxes(east_west, east_west[0:1], wet_east[None], 2, lon_count)
        north_south = fold_rows(level_fields, 3, field_parity, seam_partner_index)
        wet_north = fold_rows(wet_mask, 3, 1.0, seam_partner_index)
        flux_north, speed_north = face_fluxes(north_south, north_south[1:2], wet_north[None], 1, lat_count)
        prognostic_rate = -(flux_east[:, :, 1:] - flux_east[:, :, :-1]) - (flux_north[:, 1:, :] - flux_north[:, :-1, :])
        spread = (speed_east[0, :, 1:] - speed_east[0, :, :-1]) + (speed_north[0, 1:, :] - speed_north[0, :-1, :])
        press_east = wrap_columns(pressure_level, 1)
        press_north = fold_rows(pressure_level, 1, 1.0, seam_partner_index)
        grad_east = 0.5 * (press_east[:, 2:] - press_east[:, :-2])
        grad_north = 0.5 * (press_north[2:, :] - press_north[:-2, :])
        return prognostic_rate, spread, grad_east, grad_north

    prognostic_rate, spread, grad_east, grad_north = lax.map(horizontal, (prognostic_bundle, submerged_indicator, pressure))
    upward = -jnp.flip(jnp.cumsum(jnp.flip(spread, 0), axis=0), 0)
    interior = COURANT * upward[1:, None] * 0.5 * (prognostic_bundle[:-1] + prognostic_bundle[1:])
    boundary = jnp.zeros((1,) + interior.shape[1:], jnp.float32)
    vertical_flux = jnp.concatenate([boundary, interior, boundary], axis=0)
    prognostic_rate = prognostic_rate - (vertical_flux[:-1] - vertical_flux[1:])

    force_zonal = prognostic_rate[:, 0] + coriolis * poleward_speed_units - PRESSURE_GAIN * grad_east
    force_merid = prognostic_rate[:, 1] - coriolis * crosswise_speed_units - PRESSURE_GAIN * grad_north
    column = jnp.maximum(submerged_layer_tally, 1).astype(jnp.float32)
    mean_zonal = jnp.sum(submerged_indicator * force_zonal, axis=0) / column
    mean_merid = jnp.sum(submerged_indicator * force_merid, axis=0) / column
    thickness = submerged_layer_tally.astype(jnp.float32) / levels

    def substep(wave_state, unused):
        sea_level, zonal_flow, merid_flow = wave_state
        mass_east = wrap_columns(thickness * zonal_flow, 1)
        mass_north = fold_rows(thickness * merid_flow, 1, -1.0, seam_partner_index)
        spread_wave = 0.5 * (mass_east[:, 2:] - mass_east[:, :-2]) + 0.5 * (mass_north[2:, :] - mass_north[:-2, :])
        next_level = wet_column * (sea_level - WAVE_MASS * spread_wave)
        level_east = wrap_columns(next_level, 1)
        level_north = fold_rows(next_level, 1, 1.0, seam_partner_index)
        next_zonal = wet_column * (zonal_flow - WAVE_MOMENTUM * 0.5 * (level_east[:, 2:] - level_east[:, :-2]) + (coriolis * merid_flow + mean_zonal) / SUBSTEPS)
        next_merid = wet_column * (merid_flow - WAVE_MOMENTUM * 0.5 * (level_north[2:, :] - level_north[:-2, :]) + (-coriolis * zonal_flow + mean_merid) / SUBSTEPS)
        return (next_level, next_zonal, next_merid), None

    final_state, unused = lax.scan(substep, (freeboard_elevation, barotropic_zonal_flow, barotropic_meridional_flow), None, length=SUBSTEPS)
    freeboard_final, barotropic_zonal_final, barotropic_meridional_final = final_state
    zonal_speed_final = submerged_indicator * (crosswise_speed_units + force_zonal - mean_zonal + (barotropic_zonal_final - barotropic_zonal_flow))
    poleward_speed_final = submerged_indicator * (poleward_speed_units + force_merid - mean_merid + (barotropic_meridional_final - barotropic_meridional_flow))
    thermal_final = submerged_indicator * (thermal_anomaly + prognostic_rate[:, 2])
    saltiness_final = submerged_indicator * (saltiness_anomaly + prognostic_rate[:, 3])
    return (zonal_speed_final, poleward_speed_final, thermal_final, saltiness_final, freeboard_final, barotropic_zonal_final, barotropic_meridional_final)
```

```python
import functools

import jax
import jax.numpy as jnp
from jax import lax
from jax.experimental import pallas as pl
from jax.experimental.pallas import tpu as pltpu
from jax.sharding import PartitionSpec as P

SUBSTEPS = 12
COURANT = 0.15
PRESSURE_GAIN = 0.1
CORIOLIS = 0.3
WAVE_MASS = 1.2
WAVE_MOMENTUM = 1.2
EPSILON = 1e-06

LANES = 128
SUB = 8
SLOT = 32
DEEP = 3
FIELDS = 4
MARGIN = 2 * SUBSTEPS


def lane_of(shape):
    return lax.broadcasted_iota(jnp.int32, shape, len(shape) - 1)


def wide_roll(values, offset):
    width = values.shape[-1]
    return pltpu.roll(values, (-offset) % width, values.ndim - 1)


def four_slots(parts, source_lane, lane):
    packed = None
    for k, part in enumerate(parts):
        moved = pltpu.roll(part, (SLOT * k - source_lane) % LANES, part.ndim - 1)
        packed = moved if packed is None else jnp.where(lane >= SLOT * k, moved, packed)
    return packed


def pack_kernel(u, v, t, s, sea, zonal, merid, tally, east, west):
    levels, rows, cols = u.shape
    lane = lane_of((SUB, LANES))
    lo, hi = slice(0, LANES), slice(cols - LANES, cols)
    for g in range(rows // SUB):
        row = slice(SUB * g, SUB * (g + 1))
        for out, where, first in ((east, hi, LANES - SLOT), (west, lo, 0)):
            for k in range(levels):
                parts = [q[k, row, where] for q in (u, v, t, s)]
                out[k, row, :] = four_slots(parts, first, lane)
            parts = [q[row, where] for q in (sea, zonal, merid)]
            parts.append(tally[row, where].astype(jnp.float32))
            out[levels, row, :] = four_slots(parts, first, lane)


def halo_tile(from_east, from_west, k, lane):
    east = pltpu.roll(from_east, (-SLOT * k) % LANES, 1)
    west = pltpu.roll(from_west, (LANES - SLOT - SLOT * k) % LANES, 1)
    return jnp.where(lane < SLOT, east, jnp.where(lane >= LANES - SLOT, west, 0.0))


def widen_kernel(
    u, v, t, s, sea, zonal, merid, tally, from_west, from_east, fields, flat, msg_a, msg_b
):
    levels, rows, cols = u.shape
    lane = lane_of((SUB, LANES))
    own, halo = slice(0, cols), slice(cols, cols + LANES)
    for g in range(rows // SUB):
        row = slice(SUB * g, SUB * (g + 1))
        for k, q in enumerate((u, v, t, s)):
            fields[k, row, :, own] = jnp.swapaxes(q[:, row, :], 0, 1)
            tiles = [halo_tile(from_east[i, row, :], from_west[i, row, :], k, lane) for i in range(levels)]
            fields[k, row, :, halo] = jnp.swapaxes(jnp.stack(tiles), 0, 1)
        for k, q in enumerate((sea, zonal, merid, tally)):
            flat[k, row, own] = q[row, :].astype(jnp.float32)
            flat[k, row, halo] = halo_tile(from_east[levels, row, :], from_west[levels, row, :], k, lane)
    even = lax.rem(lax.axis_index("lat"), 2) == 0

    def fill(msg, first):
        for k in range(FIELDS):
            for q in range(DEEP):
                msg[k * DEEP + q] = fields[k, first + q]
        msg[FIELDS * DEEP, 0:DEEP, :] = flat[3, first : first + DEEP, :]
        msg[FIELDS * DEEP, DEEP:SUB, :] = jnp.zeros((SUB - DEEP, flat.shape[2]), jnp.float32)

    @pl.when(even)
    def _():
        fill(msg_a, rows - DEEP)
        fill(msg_b, 0)

    @pl.when(jnp.logical_not(even))
    def _():
        fill(msg_a, 0)
        fill(msg_b, rows - DEEP)


def across_fold(near, far, offset, lane):
    cols = near.shape[1] - LANES
    count = cols // LANES
    tiles = [far[:, cols:]] + [far[:, LANES * i : LANES * (i + 1)] for i in range(count)]
    tiles += [near[:, LANES * i : LANES * (i + 1)] for i in range(count)] + [near[:, cols:]]
    back = LANES - 1 - lane
    tiles = [jnp.take_along_axis(x, back, axis=1) for x in tiles[::-1]]
    amount = cols + LANES - 1 - offset
    tile, part = lax.div(amount, LANES), lax.rem(amount, LANES)
    moved = []
    for k in range(count + 3):
        value = tiles[k]
        for first in range(1, count):
            value = jnp.where(tile == first + 1, tiles[k + first], value)
        moved.append(pltpu.roll(value, LANES - part, 1))
    keep = lane < LANES - part
    out = [jnp.where(keep, moved[k], moved[k + 1]) for k in range(count + 2)]
    last = jnp.where(lane < SLOT, out[count + 1], jnp.where(lane >= LANES - SLOT, out[0], 0.0))
    return jnp.concatenate(out[1 : count + 1] + [last], axis=1)


def weno_flux(speed, low2, low1, here, up1, up2, up3):
    ahead = speed >= 0.0
    a = jnp.where(ahead, low2, up3)
    b = jnp.where(ahead, low1, up2)
    c = jnp.where(ahead, here, up1)
    d = jnp.where(ahead, up1, here)
    e = jnp.where(ahead, up2, low1)
    g0, g1, g2, g3 = b - a, c - b, d - c, e - d
    third = 13.0 / 3.0

    def smooth(curve, slope):
        total = (4.0 * EPSILON + slope * slope) + third * (curve * curve)
        return total * total

    q0 = smooth(g1 - g0, 3.0 * g1 - g0)
    q1 = smooth(g2 - g1, g1 + g2)
    q2 = smooth(g3 - g2, g3 - 3.0 * g2)
    w0 = q1 * q2
    w1 = 6.0 * (q0 * q2)
    w2 = 3.0 * (q0 * q1)
    top = w0 * (5.0 * g1 - 2.0 * g0) + w1 * (g1 + 2.0 * g2) + w2 * (4.0 * g2 - g3)
    face = c + top / (6.0 * (w0 + w1 + w2))
    return COURANT * speed * face


def level_sums(values, level, upwards):
    for step in (1, 2, 4):
        moved = pltpu.roll(values, SUB - step if upwards else step, 0)
        inside = level < SUB - step if upwards else level >= step
        values = values + jnp.where(inside, moved, 0.0)
    return values


def flux_kernel(
    sizes,
    seam,
    fields,
    flat,
    got_a,
    got_b,
    got_c,
    tracer_t,
    tracer_s,
    base_u,
    base_v,
    six,
    south,
    north,
    wet,
    speed_n,
    speed_e,
    flux_n,
    press,
    final,
):
    rows, lat_size = sizes
    cols = tracer_t.shape[2]
    width = cols + LANES
    lat = lax.axis_index("lat")
    even = lax.rem(lat, 2) == 0
    top = lat == lat_size - 1
    lane = lane_of((SUB, LANES))
    planes = FIELDS * DEEP

    @pl.when(even)
    def _():
        south[...] = got_b[...]
        north[...] = got_a[...]

    @pl.when(jnp.logical_not(even))
    def _():
        south[...] = got_a[...]

    @pl.when(jnp.logical_not(even) & jnp.logical_not(top))
    def _():
        north[...] = got_b[...]

    @pl.when(top)
    def _():
        offset = lax.rem(seam[0], cols)
        for k in range(FIELDS):
            for q in range(DEEP):
                ghost = across_fold(got_b[k * DEEP + q], got_c[k * DEEP + q], offset, lane)
                north[k * DEEP + DEEP - 1 - q] = -ghost if k < 2 else ghost
        ghost = across_fold(got_b[planes], got_c[planes], offset, lane)
        north[planes, 0:1, :] = ghost[DEEP - 1 : DEEP, :]

    def row_of(k, j, at):
        if j < DEEP:
            return south[k * DEEP + j, :, at]
        if j < DEEP + rows:
            return fields[k, j - DEEP, :, at]
        return north[k * DEEP + j - DEEP - rows, :, at]

    level = lax.broadcasted_iota(jnp.int32, (SUB, width), 0)
    level_real = level.astype(jnp.float32)
    every = slice(None)

    def set_wet(index, tally_row):
        wet[index] = (level_real < jnp.broadcast_to(tally_row, (SUB, width))).astype(jnp.float32)

    set_wet(0, south[planes, DEEP - 1 : DEEP, :])
    for j in range(rows):
        set_wet(j + 1, flat[3, j : j + 1, :])
    set_wet(rows + 1, north[planes, 0:1, :])

    for j in range(rows + 1):
        speed = row_of(1, j + 2, every) + row_of(1, j + 3, every)
        speed_n[j] = 0.5 * speed * wet[j] * wet[j + 1]
    for j in range(rows + 2):
        density = 0.8 * row_of(3, j + 2, every) - 0.2 * row_of(2, j + 2, every)
        press[j] = level_sums(density, level, False) - 0.5 * density

    def north_fluxes(index, carry):
        k, tile = lax.div(index, width // LANES), lax.rem(index, width // LANES)
        at = pl.ds(pl.multiple_of(tile * LANES, LANES), LANES)
        window = [row_of(k, j, at) for j in range(5)]
        for j in range(rows + 1):
            window.append(row_of(k, j + 5, at))
            flux_n[k, j, :, at] = weno_flux(speed_n[j, :, at], *window)
            window.pop(0)
        return carry

    lax.fori_loop(0, FIELDS * (width // LANES), north_fluxes, 0)

    total_rows = rows * lat_size

    def one_row(j, carry):
        mask = wet[j + 1]
        u = fields[0, j]
        speed = 0.5 * (u + wide_roll(u, 1)) * mask * wide_roll(mask, 1)
        spread = speed - wide_roll(speed, -1) + (speed_n[j + 1] - speed_n[j])
        upward = -level_sums(spread, level, True)
        rise = jnp.where(level >= 1, (0.5 * COURANT) * upward, 0.0)
        rates = []
        for k in range(FIELDS):
            q = fields[k, j]
            flux = weno_flux(
                speed,
                wide_roll(q, -2),
                wide_roll(q, -1),
                q,
                wide_roll(q, 1),
                wide_roll(q, 2),
                wide_roll(q, 3),
            )
            vertical = rise * (q + pltpu.roll(q, 1, 0))
            below = pltpu.roll(vertical, SUB - 1, 0)
            rates.append(
                -(flux - wide_roll(flux, -1))
                - (flux_n[k, j + 1] - flux_n[k, j])
                - (vertical - below)
            )
        place = (lat * rows + j).astype(jnp.float32)
        coriolis = CORIOLIS * (2.0 * (place + 0.5) / total_rows - 1.0)
        v = fields[1, j]
        pressure = press[j + 1]
        grad_east = 0.5 * (wide_roll(pressure, 1) - wide_roll(pressure, -1))
        grad_north = 0.5 * (press[j + 2] - press[j])
        force_u = rates[0] + coriolis * v - PRESSURE_GAIN * grad_east
        force_v = rates[1] - coriolis * u - PRESSURE_GAIN * grad_north
        depth = jnp.maximum(flat[3, pl.ds(j, 1), :], 1.0)
        six[4, pl.ds(j, 1), :] = jnp.sum(mask * force_u, axis=0, keepdims=True) / depth
        six[5, pl.ds(j, 1), :] = jnp.sum(mask * force_v, axis=0, keepdims=True) / depth
        base_u[j] = (u + force_u)[:, :cols]
        base_v[j] = (v + force_v)[:, :cols]
        for k in (2, 3):
            final[k - 2, j] = (mask * (fields[k, j] + rates[k]))[:, :cols]
        return carry

    lax.fori_loop(0, rows, one_row, 0)
    for g in range(rows // SUB):
        row = slice(SUB * g, SUB * (g + 1))
        tracer_t[:, row, :] = jnp.swapaxes(final[0, row], 0, 1)
        tracer_s[:, row, :] = jnp.swapaxes(final[1, row], 0, 1)
    six[0:4] = flat[...]


def pair_kernel(sizes, six, got_a, msg_1, msg_2):
    rows, lat_size = sizes
    lat = lax.axis_index("lat")
    even = lax.rem(lat, 2) == 0
    pair_even = lax.rem(lax.div(lat, 2), 2) == 0
    rest = MARGIN - rows

    def last(msg, lower, upper):
        msg[:, 0:rest, :] = lower[:, rows - rest : rows, :]
        msg[:, rest:MARGIN, :] = upper[...]

    def first(msg, lower, upper):
        msg[:, 0:rows, :] = lower[...]
        msg[:, rows:MARGIN, :] = upper[:, 0:rest, :]

    for bottom, lower, upper in ((True, six, got_a), (False, got_a, six)):
        for which in (True, False):
            here = (even if bottom else jnp.logical_not(even)) & (
                pair_even if which else jnp.logical_not(pair_even)
            )

            @pl.when(here)
            def _(lower=lower, upper=upper, which=which):
                (last if which else first)(msg_1, lower, upper)
                (first if which else last)(msg_2, lower, upper)


def wave_kernel(
    sizes,
    seam,
    six,
    got_a,
    got_1,
    got_2,
    got_f,
    base_u,
    base_v,
    out_u,
    out_v,
    out_sea,
    out_zonal,
    out_merid,
    space,
):
    rows, levels, lat_size = sizes
    cols = out_sea.shape[1]
    width = cols + LANES
    lat = lax.axis_index("lat")
    even = lax.rem(lat, 2) == 0
    pair = lax.div(lat, 2)
    pair_even = lax.rem(pair, 2) == 0
    top = pair == lat_size // 2 - 1
    lane = lane_of((SUB, LANES))
    own_low = slice(MARGIN, MARGIN + rows)
    own_high = slice(MARGIN + rows, MARGIN + 2 * rows)
    below, above = slice(0, MARGIN), slice(MARGIN + 2 * rows, 2 * MARGIN + 2 * rows)

    @pl.when(even)
    def _():
        space[:, own_low, :] = six[...]
        space[:, own_high, :] = got_a[...]

    @pl.when(jnp.logical_not(even))
    def _():
        space[:, own_low, :] = got_a[...]
        space[:, own_high, :] = six[...]

    @pl.when(pair_even)
    def _():
        space[:, below, :] = got_2[...]
        space[:, above, :] = got_1[...]

    @pl.when(jnp.logical_not(pair_even))
    def _():
        space[:, below, :] = got_1[...]

    @pl.when(jnp.logical_not(pair_even) & jnp.logical_not(top))
    def _():
        space[:, above, :] = got_2[...]

    @pl.when(top)
    def _():
        offset = lax.rem(seam[0], cols)
        turn = SUB - 1 - lax.broadcasted_iota(jnp.int32, (SUB, LANES), 0)
        for k, parity in enumerate((1.0, -1.0, -1.0, 1.0, -1.0, -1.0)):
            for g in range(MARGIN // SUB):
                row = slice(SUB * g, SUB * (g + 1))
                ghost = across_fold(got_2[k, row, :], got_f[k, row, :], offset, lane)
                place = above.start + MARGIN - SUB * (g + 1)
                for i in range(width // LANES):
                    part = jnp.take_along_axis(ghost[:, LANES * i : LANES * (i + 1)], turn, axis=0)
                    space[k, place : place + SUB, LANES * i : LANES * (i + 1)] = parity * part

    height = rows + 2 * MARGIN
    window = pl.ds(pl.multiple_of(jnp.where(even, 0, rows), SUB), height)
    tally = space[3, window, :]
    wet = (tally > 0.0).astype(jnp.float32)
    thick = (0.5 * WAVE_MASS / levels) * tally
    total_rows = rows * lat_size
    place = lax.broadcasted_iota(jnp.int32, (height, width), 0) + (lat * rows - MARGIN)
    place = jnp.minimum(place, 2 * total_rows - 1 - place).astype(jnp.float32)
    turning = (CORIOLIS / SUBSTEPS) * (2.0 * (place + 0.5) / total_rows - 1.0)
    push_u = space[4, window, :] * (1.0 / SUBSTEPS)
    push_v = space[5, window, :] * (1.0 / SUBSTEPS)

    def step(index, state):
        sea, zonal, merid = state
        mass_e, mass_n = thick * zonal, thick * merid
        spread = (wide_roll(mass_e, 1) - wide_roll(mass_e, -1)) + (
            pltpu.roll(mass_n, height - 1, 0) - pltpu.roll(mass_n, 1, 0)
        )
        sea = wet * (sea - spread)
        slope_e = wide_roll(sea, 1) - wide_roll(sea, -1)
        slope_n = pltpu.roll(sea, height - 1, 0) - pltpu.roll(sea, 1, 0)
        half = 0.5 * WAVE_MOMENTUM
        next_zonal = wet * (zonal - half * slope_e + (turning * merid + push_u))
        next_merid = wet * (merid - half * slope_n + (push_v - turning * zonal))
        return sea, next_zonal, next_merid

    start = (space[0, window, :], space[1, window, :], space[2, window, :])
    sea, zonal, merid = lax.fori_loop(0, SUBSTEPS, step, start)
    mine = slice(MARGIN, MARGIN + rows)
    out_sea[...] = sea[mine, :cols]
    out_zonal[...] = zonal[mine, :cols]
    out_merid[...] = merid[mine, :cols]
    level = lax.broadcasted_iota(jnp.int32, (SUB, cols), 0).astype(jnp.float32)
    for base, flow, final, start_of, mean in (
        (base_u, out_u, out_zonal, 1, 4),
        (base_v, out_v, out_merid, 2, 5),
    ):
        for g in range(rows // SUB):
            block = []
            for j in range(SUB * g, SUB * (g + 1)):
                row = slice(j, j + 1)
                mask = level < jnp.broadcast_to(six[3, row, :cols], (SUB, cols))
                change = final[row, :] - six[start_of, row, :cols] - six[mean, row, :cols]
                block.append(mask.astype(jnp.float32) * (base[j] + jnp.broadcast_to(change, (SUB, cols))))
            flow[:, SUB * g : SUB * (g + 1), :] = jnp.swapaxes(jnp.stack(block), 0, 1)


def real(*shape):
    return jax.ShapeDtypeStruct(shape, jnp.float32)


def call(kernel, outs, scratch=(), seam=False):
    vmem = pl.BlockSpec(memory_space=pltpu.VMEM)

    def run(*args):
        specs = [vmem] * len(args)
        if seam:
            specs[0] = pl.BlockSpec(memory_space=pltpu.SMEM)
        return pl.pallas_call(
            kernel,
            out_shape=outs,
            in_specs=specs,
            out_specs=jax.tree.map(lambda _: vmem, outs),
            scratch_shapes=[pltpu.VMEM(shape, jnp.float32) for shape in scratch],
        )(*args)

    return run


def on_device(lon_size, lat_size, *arguments):
    u, v, t, s, sea, zonal, merid, tally, seam = arguments
    levels, rows, cols = u.shape
    width = cols + LANES
    assert levels == SUB and rows % SUB == 0 and lat_size % 4 == 0
    tile = lax.rem(lax.div(seam[0], cols) + lax.axis_index("lon"), lon_size)

    def moves(lats, fold=(), turn=0):
        pairs = [(x * lat_size + a, x * lat_size + b) for a, b in lats for x in range(lon_size)]
        for a in fold:
            pairs += [(x * lat_size + a, (turn - x) % lon_size * lat_size + a) for x in range(lon_size)]
        return pairs

    def send(values, pairs):
        return lax.ppermute(values, ("lon", "lat"), pairs)

    def both(pairs):
        return [p for a, b in pairs for p in ((a, b), (b, a))]

    ring = [(i, (i + 1) % lon_size) for i in range(lon_size)]
    inside = both((a, a + 1) for a in range(0, lat_size, 2))
    between = both((a, a + 1) for a in range(1, lat_size - 1, 2))
    chips = lat_size // 2
    chips_1 = both((2 * c + b, 2 * c + 2 + b) for c in range(0, chips - 1, 2) for b in (0, 1))
    chips_2 = both((2 * c + b, 2 * c + 2 + b) for c in range(1, chips - 1, 2) for b in (0, 1))
    last, last_two = (lat_size - 1,), (lat_size - 2, lat_size - 1)

    message = real(levels + 1, rows, LANES)
    flat_args = (u, v, t, s, sea, zonal, merid, tally)
    east, west = call(pack_kernel, (message, message))(*flat_args)
    from_west = lax.ppermute(east, "lon", ring)
    from_east = lax.ppermute(west, "lon", [(b, a) for a, b in ring])

    deep = real(FIELDS * DEEP + 1, SUB, width)
    fields, flat, msg_a, msg_b = call(
        widen_kernel,
        (real(FIELDS, rows, SUB, width), real(FIELDS, rows, width), deep, deep),
    )(*flat_args, from_west, from_east)

    def deep_exchange(turn):
        def run(a, b):
            return (
                send(a, moves(inside)),
                send(b, moves(between, last, turn)),
                send(b, moves((), last, turn - 1)),
            )

        return run

    got_a, got_b, got_c = lax.switch(tile, [deep_exchange(i) for i in range(lon_size)], msg_a, msg_b)

    base = real(rows, SUB, cols)
    tracer = real(levels, rows, cols)
    tracer_t, tracer_s, base_u, base_v, six = call(
        functools.partial(flux_kernel, (rows, lat_size)),
        (tracer, tracer, base, base, real(6, rows, width)),
        scratch=(
            deep.shape,
            deep.shape,
            (rows + 2, SUB, width),
            (rows + 1, SUB, width),
            (rows, SUB, width),
            (FIELDS, rows + 1, SUB, width),
            (rows + 2, SUB, width),
            (2, rows, SUB, cols),
        ),
        seam=True,
    )(seam, fields, flat, got_a, got_b, got_c)

    got_pair = send(six, moves(inside))
    strip = real(6, MARGIN, width)
    msg_1, msg_2 = call(functools.partial(pair_kernel, (rows, lat_size)), (strip, strip))(six, got_pair)

    def strip_exchange(turn):
        def run(a, b):
            return (
                send(a, moves(chips_1)),
                send(b, moves(chips_2, last_two, turn)),
                send(b, moves((), last_two, turn - 1)),
            )

        return run

    got_1, got_2, got_f = lax.switch(tile, [strip_exchange(i) for i in range(lon_size)], msg_1, msg_2)
    plane = real(rows, cols)
    out_u, out_v, out_sea, out_zonal, out_merid = call(
        functools.partial(wave_kernel, (rows, levels, lat_size)),
        (tracer, tracer, plane, plane, plane),
        scratch=((6, 2 * rows + 2 * MARGIN, width),),
        seam=True,
    )(seam, six, got_pair, got_1, got_2, got_f, base_u, base_v)
    return out_u, out_v, tracer_t, tracer_s, out_sea, out_zonal, out_merid


def solution(mesh):
    deep, plane = P(None, "lat", "lon"), P("lat", "lon")
    return jax.shard_map(
        functools.partial(on_device, mesh.shape["lon"], mesh.shape["lat"]),
        mesh=mesh,
        in_specs=(deep,) * 4 + (plane,) * 4 + (P("lon"),),
        out_specs=(deep,) * 4 + (plane,) * 3,
        check_vma=False,
    )
```

```python
import functools

import jax
import jax.numpy as jnp
from jax import lax
from jax.experimental import pallas as pl
from jax.experimental.pallas import tpu as pltpu
from jax.sharding import PartitionSpec as P

SUBSTEPS = 12
COURANT = 0.15
PRESSURE_GAIN = 0.1
CORIOLIS = 0.3
WAVE_MASS = 1.2
WAVE_MOMENTUM = 1.2
EPSILON = 1e-06

LANES = 128
SUB = 8
SLOT = 32
DEEP = 3
FIELDS = 4
MARGIN = 2 * SUBSTEPS


def lane_of(shape):
    return lax.broadcasted_iota(jnp.int32, shape, len(shape) - 1)


def wide_roll(values, offset):
    width = values.shape[-1]
    return pltpu.roll(values, (-offset) % width, values.ndim - 1)


def half_tiles(cols):
    assert cols == 2 * LANES
    return slice(0, LANES), slice(LANES, cols)


def own_slot(packed, k, first):
    return pltpu.roll(packed, lax.rem(first - SLOT * k + 2 * LANES, LANES), packed.ndim - 1)


def four_slots(parts, source_lane, lane):
    packed = None
    for k, part in enumerate(parts):
        moved = pltpu.roll(part, lax.rem(SLOT * k - source_lane + LANES, LANES), part.ndim - 1)
        packed = moved if packed is None else jnp.where(lane >= SLOT * k, moved, packed)
    return packed


def pack_kernel(u, v, t, s, sea, zonal, merid, tally, east, west):
    levels, rows, cols = u.shape
    lane = lane_of((SUB, LANES))
    lo, hi = slice(0, LANES), slice(cols - LANES, cols)
    for g in range(rows // SUB):
        row = slice(SUB * g, SUB * (g + 1))
        for out, where, first in ((east, hi, LANES - SLOT), (west, lo, 0)):
            for k in range(levels):
                parts = [q[k, row, where] for q in (u, v, t, s)]
                out[k, row, :] = four_slots(parts, first, lane)
            parts = [q[row, where] for q in (sea, zonal, merid)]
            parts.append(tally[row, where].astype(jnp.float32))
            out[levels, row, :] = four_slots(parts, first, lane)


def halo_tile(from_east, from_west, k, lane):
    east = pltpu.roll(from_east, (-SLOT * k) % LANES, 1)
    west = pltpu.roll(from_west, (LANES - SLOT - SLOT * k) % LANES, 1)
    return jnp.where(lane < SLOT, east, jnp.where(lane >= LANES - SLOT, west, 0.0))


def widen_kernel(
    top_lat,
    seam,
    u,
    v,
    t,
    s,
    sea,
    zonal,
    merid,
    tally,
    from_west,
    from_east,
    fields,
    flat,
    msg_a,
    msg_b,
    msg_c,
):
    levels, rows, cols = u.shape
    lane = lane_of((SUB, LANES))
    own, halo = slice(0, cols), slice(cols, cols + LANES)
    for g in range(rows // SUB):
        row = slice(SUB * g, SUB * (g + 1))
        for k, q in enumerate((u, v, t, s)):
            fields[k, row, :, own] = jnp.swapaxes(q[:, row, :], 0, 1)
            tiles = [halo_tile(from_east[i, row, :], from_west[i, row, :], k, lane) for i in range(levels)]
            fields[k, row, :, halo] = jnp.swapaxes(jnp.stack(tiles), 0, 1)
        for k, q in enumerate((sea, zonal, merid, tally)):
            flat[k, row, own] = q[row, :].astype(jnp.float32)
            flat[k, row, halo] = halo_tile(from_east[levels, row, :], from_west[levels, row, :], k, lane)
    even = lax.rem(lax.axis_index("lat"), 2) == 0

    def fill(msg, first):
        for k in range(FIELDS):
            for q in range(DEEP):
                msg[k * DEEP + q] = fields[k, first + q]
        msg[FIELDS * DEEP, 0:DEEP, :] = flat[3, first : first + DEEP, :]
        msg[FIELDS * DEEP, DEEP:SUB, :] = jnp.zeros((SUB - DEEP, flat.shape[2]), jnp.float32)

    @pl.when(even)
    def _():
        fill(msg_a, rows - DEEP)
        fill(msg_b, 0)

    @pl.when(jnp.logical_not(even))
    def _():
        fill(msg_a, 0)
        fill(msg_b, rows - DEEP)

    @pl.when(lax.axis_index("lat") == top_lat)
    def _():
        west, _ = fold_offset(seam, cols)
        first = jnp.where(west, LANES - SLOT, 0)
        for q in range(DEEP):
            edges = []
            for k in range(FIELDS):
                low, high = (fields[k, rows - DEEP + q, :, at] for at in half_tiles(cols))
                msg_c[k * DEEP + q] = jnp.where(west, high, low)
                edges.append(jnp.where(west, low, high))
            msg_c[FIELDS * DEEP + q] = four_slots(edges, first, lane)
        low, high = (msg_b[FIELDS * DEEP, :, at] for at in half_tiles(cols))
        msg_c[(FIELDS + 1) * DEEP] = jnp.where(west, high, low)
        msg_c[(FIELDS + 1) * DEEP + 1] = jnp.where(west, low, high)


def fold_offset(seam, cols):
    rest = lax.rem(seam[0], cols)
    return rest >= cols // 2, lax.rem(rest, LANES)


def across_fold(line, rest, lane):
    back = LANES - 1 - lane
    part = LANES - 1 - rest
    moved = [
        pltpu.roll(jnp.take_along_axis(x, back, axis=1), LANES - part, 1) for x in line[::-1]
    ]
    keep = lane < LANES - part
    out = [jnp.where(keep, p, q) for p, q in zip(moved, moved[1:])]
    last = jnp.where(lane < SLOT, out[-1], jnp.where(lane >= LANES - SLOT, out[0], 0.0))
    return out[1:-1] + [last]


def facing_line(west, whole, edge, half, half_edge):
    from_west = [half_edge, half] + whole + [edge]
    from_east = [edge] + whole + [half, half_edge]
    return [jnp.where(west, p, q) for p, q in zip(from_west, from_east)]


def weno_flux(speed, low2, low1, here, up1, up2, up3):
    ahead = speed >= 0.0
    a = jnp.where(ahead, low2, up3)
    b = jnp.where(ahead, low1, up2)
    c = jnp.where(ahead, here, up1)
    d = jnp.where(ahead, up1, here)
    e = jnp.where(ahead, up2, low1)
    g0, g1, g2, g3 = b - a, c - b, d - c, e - d
    third = 13.0 / 3.0

    def smooth(curve, slope):
        total = (4.0 * EPSILON + slope * slope) + third * (curve * curve)
        return total * total

    q0 = smooth(g1 - g0, 3.0 * g1 - g0)
    q1 = smooth(g2 - g1, g1 + g2)
    q2 = smooth(g3 - g2, g3 - 3.0 * g2)
    w0 = q1 * q2
    w1 = 6.0 * (q0 * q2)
    w2 = 3.0 * (q0 * q1)
    top = w0 * (5.0 * g1 - 2.0 * g0) + w1 * (g1 + 2.0 * g2) + w2 * (4.0 * g2 - g3)
    face = c + top / (6.0 * (w0 + w1 + w2))
    return COURANT * speed * face


def level_sums(values, level, upwards):
    for step in (1, 2, 4):
        moved = pltpu.roll(values, SUB - step if upwards else step, 0)
        inside = level < SUB - step if upwards else level >= step
        values = values + jnp.where(inside, moved, 0.0)
    return values


def row_of(k, j, at, rows, fields, south, north):
    if j < DEEP:
        return south[k * DEEP + j, :, at]
    if j < DEEP + rows:
        return fields[k, j - DEEP, :, at]
    return north[k * DEEP + j - DEEP - rows, :, at]


def north_fluxes(index, first, tiles, rows, fields, south, north, speed_n, flux_n):
    k, tile = lax.div(index, tiles), lax.rem(index, tiles)
    at = pl.ds(pl.multiple_of(tile * LANES, LANES), LANES)
    window = [row_of(first + k, j, at, rows, fields, south, north) for j in range(5)]
    for j in range(rows + 1):
        window.append(row_of(first + k, j + 5, at, rows, fields, south, north))
        flux_n[k, j, :, at] = weno_flux(speed_n[j, :, at], *window)
        window.pop(0)


def row_rate(q, speed, rise, north_step):
    flux = weno_flux(speed, *(wide_roll(q, i) if i else q for i in range(-2, 4)))
    vertical = rise * (q + pltpu.roll(q, 1, 0))
    below = pltpu.roll(vertical, SUB - 1, 0)
    return -(flux - wide_roll(flux, -1)) - north_step - (vertical - below)


def force_kernel(
    sizes,
    seam,
    fields,
    flat,
    got_a,
    got_b,
    got_c,
    base_u,
    base_v,
    six,
    south,
    north,
    speed_n,
    speed_e,
    rises,
    wet,
    flux_n,
    press,
):
    rows, lat_size = sizes
    cols = base_u.shape[2]
    width = cols + LANES
    lat = lax.axis_index("lat")
    even = lax.rem(lat, 2) == 0
    top = lat == lat_size - 1
    lane = lane_of((SUB, LANES))
    planes = FIELDS * DEEP

    @pl.when(even)
    def _():
        south[...] = got_b[...]
        north[...] = got_a[...]

    @pl.when(jnp.logical_not(even))
    def _():
        south[...] = got_a[...]

    @pl.when(jnp.logical_not(even) & jnp.logical_not(top))
    def _():
        north[...] = got_b[...]

    @pl.when(top)
    def _():
        west, rest = fold_offset(seam, cols)
        first = jnp.where(west, LANES - SLOT, 0)
        tiles = [slice(LANES * i, LANES * (i + 1)) for i in range(width // LANES)]

        def ghosts(plane, half, half_edge):
            parts = [got_b[plane, :, at] for at in tiles]
            line = facing_line(west, parts[:-1], parts[-1], half, half_edge)
            return across_fold(line, rest, lane)

        for k in range(FIELDS):
            for q in range(DEEP):
                plane = k * DEEP + q
                edge = own_slot(got_c[planes + q], k, first)
                for at, ghost in zip(tiles, ghosts(plane, got_c[plane], edge)):
                    north[k * DEEP + DEEP - 1 - q, :, at] = -ghost if k < 2 else ghost
        for at, ghost in zip(tiles, ghosts(planes, got_c[planes + DEEP], got_c[planes + DEEP + 1])):
            north[planes, 0:1, at] = ghost[DEEP - 1 : DEEP, :]

    level = lax.broadcasted_iota(jnp.int32, (SUB, width), 0)
    level_real = level.astype(jnp.float32)
    every = slice(None)

    def row(k, j):
        return row_of(k, j, every, rows, fields, south, north)

    def set_wet(index, tally_row):
        wet[index] = (level_real < jnp.broadcast_to(tally_row, (SUB, width))).astype(jnp.float32)

    set_wet(0, south[planes, DEEP - 1 : DEEP, :])
    for j in range(rows):
        set_wet(j + 1, flat[3, j : j + 1, :])
    set_wet(rows + 1, north[planes, 0:1, :])

    for j in range(rows + 1):
        speed_n[j] = 0.5 * (row(1, j + 2) + row(1, j + 3)) * wet[j] * wet[j + 1]
    for j in range(rows + 2):
        density = 0.8 * row(3, j + 2) - 0.2 * row(2, j + 2)
        press[j] = level_sums(density, level, False) - 0.5 * density

    tiles = width // LANES

    def northward(index, carry):
        north_fluxes(index, 0, tiles, rows, fields, south, north, speed_n, flux_n)
        return carry

    lax.fori_loop(0, 2 * tiles, northward, 0)
    total_rows = rows * lat_size

    def one_row(j, carry):
        mask = wet[j + 1]
        u, v = fields[0, j], fields[1, j]
        speed = 0.5 * (u + wide_roll(u, 1)) * mask * wide_roll(mask, 1)
        spread = speed - wide_roll(speed, -1) + (speed_n[j + 1] - speed_n[j])
        upward = -level_sums(spread, level, True)
        rise = jnp.where(level >= 1, (0.5 * COURANT) * upward, 0.0)
        speed_e[j] = speed
        rises[j] = rise
        rate_u = row_rate(u, speed, rise, flux_n[0, j + 1] - flux_n[0, j])
        rate_v = row_rate(v, speed, rise, flux_n[1, j + 1] - flux_n[1, j])
        place = (lat * rows + j).astype(jnp.float32)
        coriolis = CORIOLIS * (2.0 * (place + 0.5) / total_rows - 1.0)
        pressure = press[j + 1]
        grad_east = 0.5 * (wide_roll(pressure, 1) - wide_roll(pressure, -1))
        grad_north = 0.5 * (press[j + 2] - press[j])
        force_u = rate_u + coriolis * v - PRESSURE_GAIN * grad_east
        force_v = rate_v - coriolis * u - PRESSURE_GAIN * grad_north
        depth = jnp.maximum(flat[3, pl.ds(j, 1), :], 1.0)
        six[4, pl.ds(j, 1), :] = jnp.sum(mask * force_u, axis=0, keepdims=True) / depth
        six[5, pl.ds(j, 1), :] = jnp.sum(mask * force_v, axis=0, keepdims=True) / depth
        base_u[j] = (u + force_u)[:, :cols]
        base_v[j] = (v + force_v)[:, :cols]
        return carry

    lax.fori_loop(0, rows, one_row, 0)
    six[0:4] = flat[...]


def tracer_kernel(
    fields, flat, south, north, speed_n, speed_e, rises, tracer_t, tracer_s, flux_n, final
):
    rows = fields.shape[1]
    cols = tracer_t.shape[2]
    tiles = cols // LANES

    def northward(index, carry):
        north_fluxes(index, 2, tiles, rows, fields, south, north, speed_n, flux_n)
        return carry

    lax.fori_loop(0, 2 * tiles, northward, 0)
    level = lax.broadcasted_iota(jnp.int32, (SUB, cols), 0).astype(jnp.float32)
    aside = jnp.zeros((SUB, LANES), jnp.float32)

    def one_row(j, carry):
        tally = jnp.broadcast_to(flat[3, pl.ds(j, 1), pl.ds(0, cols)], (SUB, cols))
        mask = (level < tally).astype(jnp.float32)
        for k in (0, 1):
            q = fields[2 + k, j]
            step = jnp.concatenate([flux_n[k, j + 1] - flux_n[k, j], aside], axis=1)
            rate = row_rate(q, speed_e[j], rises[j], step)
            final[k, j] = mask * (q + rate)[:, :cols]
        return carry

    lax.fori_loop(0, rows, one_row, 0)
    for g in range(rows // SUB):
        row = slice(SUB * g, SUB * (g + 1))
        tracer_t[:, row, :] = jnp.swapaxes(final[0, row], 0, 1)
        tracer_s[:, row, :] = jnp.swapaxes(final[1, row], 0, 1)


def pair_kernel(sizes, seam, six, got_a, msg_1, full, full_low, half, half_low, *more):
    rows, lat_size = sizes
    cols = six.shape[2] - LANES
    lat = lax.axis_index("lat")
    even = lax.rem(lat, 2) == 0
    pair = lax.div(lat, 2)
    pair_even = lax.rem(pair, 2) == 0
    top = pair == lat_size // 2 - 1
    rest = MARGIN - rows
    lane = lane_of((SUB, LANES))

    def last(msg, lower, upper):
        msg[:, 0:rest, :] = lower[:, rows - rest : rows, :]
        msg[:, rest:MARGIN, :] = upper[...]

    def first(msg, lower, upper):
        msg[:, 0:rows, :] = lower[...]
        msg[:, rows:MARGIN, :] = upper[:, 0:rest, :]

    def across(lower, upper, low):
        whole_out, half_out = (full_low, half_low) if low else (full, half)
        west, _ = fold_offset(seam, cols)
        height = whole_out.shape[1]
        count = six.shape[0]
        for g in range(height // SUB):
            up = 2 * rows - height + SUB * g
            source, start = (lower, up) if up < rows else (upper, up - rows)
            row, out = slice(start, start + SUB), slice(SUB * g, SUB * (g + 1))
            edges, half_edges = [], []
            for k in range(count):
                left, right = (source[k, row, at] for at in half_tiles(cols))
                whole_out[2 * k, out, :] = left
                whole_out[2 * k + 1, out, :] = right
                half_out[k, out, :] = jnp.where(west, right, left)
                edges.append(source[k, row, cols:])
                half_edges.append(jnp.where(west, left, right))
            for i in range(0, count, 4):
                packed = four_slots(edges[i : i + 4], jnp.where(west, 0, LANES - SLOT), lane)
                whole_out[2 * count + i // 4, out, :] = packed
                packed = four_slots(half_edges[i : i + 4], jnp.where(west, LANES - SLOT, 0), lane)
                half_out[count + i // 4, out, :] = packed

    for bottom, lower, upper in ((True, six, got_a), (False, got_a, six)):
        mine = even if bottom else jnp.logical_not(even)

        @pl.when(mine & pair_even)
        def _(lower=lower, upper=upper):
            last(msg_1, lower, upper)
            if more:
                first(more[0], lower, upper)

        @pl.when(mine & jnp.logical_not(pair_even))
        def _(lower=lower, upper=upper):
            first(msg_1, lower, upper)
            if more:
                last(more[0], lower, upper)

        @pl.when(mine & top)
        def _(lower=lower, upper=upper, bottom=bottom):
            across(lower, upper, bottom)


def wave_kernel(
    sizes,
    seam,
    six,
    got_a,
    got_1,
    full,
    full_low,
    half,
    half_low,
    base_u,
    base_v,
    *rest,
):
    rows, levels, lat_size = sizes
    got_2 = rest[:-6]
    out_u, out_v, out_sea, out_zonal, out_merid, space = rest[-6:]
    cols = out_sea.shape[1]
    width = cols + LANES
    lat = lax.axis_index("lat")
    even = lax.rem(lat, 2) == 0
    pair = lax.div(lat, 2)
    pair_even = lax.rem(pair, 2) == 0
    top = pair == lat_size // 2 - 1
    lane = lane_of((SUB, LANES))
    own_low = slice(MARGIN, MARGIN + rows)
    own_high = slice(MARGIN + rows, MARGIN + 2 * rows)
    below, above = slice(0, MARGIN), slice(MARGIN + 2 * rows, 2 * MARGIN + 2 * rows)

    @pl.when(even)
    def _():
        space[:, own_low, :] = six[...]
        space[:, own_high, :] = got_a[...]

    @pl.when(jnp.logical_not(even))
    def _():
        space[:, own_low, :] = got_a[...]
        space[:, own_high, :] = six[...]

    @pl.when(pair_even)
    def _():
        space[:, below, :] = got_2[0][...] if got_2 else jnp.zeros_like(got_1)
        space[:, above, :] = got_1[...]

    @pl.when(jnp.logical_not(pair_even))
    def _():
        space[:, below, :] = got_1[...]

    if got_2:

        @pl.when(jnp.logical_not(pair_even) & jnp.logical_not(top))
        def _():
            space[:, above, :] = got_2[0][...]

    def ghosts(whole, part):
        west, rest = fold_offset(seam, cols)
        turn = SUB - 1 - lax.broadcasted_iota(jnp.int32, (SUB, LANES), 0)
        count = six.shape[0]
        height = whole.shape[1]
        for k, parity in enumerate((1.0, -1.0, -1.0, 1.0, -1.0, -1.0)):
            for g in range(height // SUB):
                row = slice(SUB * g, SUB * (g + 1))
                edge = own_slot(whole[2 * count + k // 4, row, :], k % 4, jnp.where(west, 0, LANES - SLOT))
                half_edge = own_slot(part[count + k // 4, row, :], k % 4, jnp.where(west, LANES - SLOT, 0))
                tiles = [whole[2 * k, row, :], whole[2 * k + 1, row, :]]
                line = facing_line(west, tiles, edge, part[k, row, :], half_edge)
                place = above.start + height - SUB * (g + 1)
                for i, ghost in enumerate(across_fold(line, rest, lane)):
                    ghost = parity * jnp.take_along_axis(ghost, turn, axis=0)
                    space[k, place : place + SUB, LANES * i : LANES * (i + 1)] = ghost

    @pl.when(top & jnp.logical_not(even))
    def _():
        ghosts(full, half)

    @pl.when(top & even)
    def _():
        ghosts(full_low, half_low)

    height = rows + 2 * MARGIN
    window = pl.ds(pl.multiple_of(jnp.where(even, 0, rows), SUB), height)
    tally = space[3, window, :]
    wet = (tally > 0.0).astype(jnp.float32)
    thick = (0.5 * WAVE_MASS / levels) * tally
    total_rows = rows * lat_size
    place = lax.broadcasted_iota(jnp.int32, (height, width), 0) + (lat * rows - MARGIN)
    place = jnp.minimum(place, 2 * total_rows - 1 - place).astype(jnp.float32)
    turning = (CORIOLIS / SUBSTEPS) * (2.0 * (place + 0.5) / total_rows - 1.0)
    push_u = space[4, window, :] * (1.0 / SUBSTEPS)
    push_v = space[5, window, :] * (1.0 / SUBSTEPS)

    def step(index, state):
        sea, zonal, merid = state
        mass_e, mass_n = thick * zonal, thick * merid
        spread = (wide_roll(mass_e, 1) - wide_roll(mass_e, -1)) + (
            pltpu.roll(mass_n, height - 1, 0) - pltpu.roll(mass_n, 1, 0)
        )
        sea = wet * (sea - spread)
        slope_e = wide_roll(sea, 1) - wide_roll(sea, -1)
        slope_n = pltpu.roll(sea, height - 1, 0) - pltpu.roll(sea, 1, 0)
        half = 0.5 * WAVE_MOMENTUM
        next_zonal = wet * (zonal - half * slope_e + (turning * merid + push_u))
        next_merid = wet * (merid - half * slope_n + (push_v - turning * zonal))
        return sea, next_zonal, next_merid

    start = (space[0, window, :], space[1, window, :], space[2, window, :])
    sea, zonal, merid = lax.fori_loop(0, SUBSTEPS, step, start)
    mine = slice(MARGIN, MARGIN + rows)
    out_sea[...] = sea[mine, :cols]
    out_zonal[...] = zonal[mine, :cols]
    out_merid[...] = merid[mine, :cols]
    level = lax.broadcasted_iota(jnp.int32, (SUB, cols), 0).astype(jnp.float32)
    for base, flow, final, start_of, mean in (
        (base_u, out_u, out_zonal, 1, 4),
        (base_v, out_v, out_merid, 2, 5),
    ):
        for g in range(rows // SUB):
            block = []
            for j in range(SUB * g, SUB * (g + 1)):
                row = slice(j, j + 1)
                mask = level < jnp.broadcast_to(six[3, row, :cols], (SUB, cols))
                change = final[row, :] - six[start_of, row, :cols] - six[mean, row, :cols]
                block.append(mask.astype(jnp.float32) * (base[j] + jnp.broadcast_to(change, (SUB, cols))))
            flow[:, SUB * g : SUB * (g + 1), :] = jnp.swapaxes(jnp.stack(block), 0, 1)


def real(*shape):
    return jax.ShapeDtypeStruct(shape, jnp.float32)


def call(kernel, outs, scratch=(), seam=False):
    vmem = pl.BlockSpec(memory_space=pltpu.VMEM)

    def run(*args):
        specs = [vmem] * len(args)
        if seam:
            specs[0] = pl.BlockSpec(memory_space=pltpu.SMEM)
        return pl.pallas_call(
            kernel,
            out_shape=outs,
            in_specs=specs,
            out_specs=jax.tree.map(lambda _: vmem, outs),
            scratch_shapes=[pltpu.VMEM(shape, jnp.float32) for shape in scratch],
        )(*args)

    return run


def on_device(lon_size, lat_size, *arguments):
    u, v, t, s, sea, zonal, merid, tally, seam = arguments
    levels, rows, cols = u.shape
    width = cols + LANES
    assert levels == SUB and rows % SUB == 0 and lat_size % 4 == 0
    tile = lax.rem(lax.div(seam[0], cols) + lax.axis_index("lon"), lon_size)
    choice = 2 * tile + (lax.rem(seam[0], cols) >= cols // 2).astype(jnp.int32)

    def partners(chosen):
        turn, west = divmod(chosen, 2)
        return (turn, turn - 1) if west else (turn - 1, turn)

    def moves(lats, fold=(), turn=0):
        pairs = [(x * lat_size + a, x * lat_size + b) for a, b in lats for x in range(lon_size)]
        for a in fold:
            pairs += [(x * lat_size + a, (turn - x) % lon_size * lat_size + a) for x in range(lon_size)]
        return pairs

    def send(values, pairs):
        return lax.ppermute(values, ("lon", "lat"), pairs)

    def both(pairs):
        return [p for a, b in pairs for p in ((a, b), (b, a))]

    ring = [(i, (i + 1) % lon_size) for i in range(lon_size)]
    inside = both((a, a + 1) for a in range(0, lat_size, 2))
    between = both((a, a + 1) for a in range(1, lat_size - 1, 2))
    chips = lat_size // 2
    chips_1 = both((2 * c + b, 2 * c + 2 + b) for c in range(0, chips - 1, 2) for b in (0, 1))
    chips_2 = both((2 * c + b, 2 * c + 2 + b) for c in range(1, chips - 1, 2) for b in (0, 1))
    high, low = (lat_size - 1,), (lat_size - 2,)

    message = real(levels + 1, rows, LANES)
    flat_args = (u, v, t, s, sea, zonal, merid, tally)
    east, west = call(pack_kernel, (message, message))(*flat_args)
    from_west = lax.ppermute(east, "lon", ring)
    from_east = lax.ppermute(west, "lon", [(b, a) for a, b in ring])

    deep = real(FIELDS * DEEP + 1, SUB, width)
    fields, flat, msg_a, msg_b, msg_c = call(
        functools.partial(widen_kernel, lat_size - 1),
        (
            real(FIELDS, rows, SUB, width),
            real(FIELDS, rows, width),
            deep,
            deep,
            real((FIELDS + 1) * DEEP + 2, SUB, LANES),
        ),
        seam=True,
    )(seam, *flat_args, from_west, from_east)

    def deep_exchange(chosen):
        whole, half = partners(chosen)

        def run(a, b, c):
            return (
                send(a, moves(inside)),
                send(b, moves(between, high, whole)),
                send(c, moves((), high, half)),
            )

        return run

    branches = range(2 * lon_size)
    got_a, got_b, got_c = lax.switch(
        choice, [deep_exchange(i) for i in branches], msg_a, msg_b, msg_c
    )

    base = real(rows, SUB, cols)
    tracer = real(levels, rows, cols)
    wide = real(rows, SUB, width)
    base_u, base_v, six, south, north, speed_n, speed_e, rises = call(
        functools.partial(force_kernel, (rows, lat_size)),
        (base, base, real(6, rows, width), deep, deep, real(rows + 1, SUB, width), wide, wide),
        scratch=((rows + 2, SUB, width), (2, rows + 1, SUB, width), (rows + 2, SUB, width)),
        seam=True,
    )(seam, fields, flat, got_a, got_b, got_c)

    got_pair = send(six, moves(inside))
    count = six.shape[0]
    packs = -(-count // 4)
    strip = real(count, MARGIN, width)
    rest = MARGIN - rows
    strips = (strip,) + tuple(
        real(planes, height, LANES)
        for planes in (2 * count + packs, count + packs)
        for height in (MARGIN, rest)
    )
    strips += (strip,) * bool(chips_2)
    messages = call(functools.partial(pair_kernel, (rows, lat_size)), strips, seam=True)(
        seam, six, got_pair
    )
    tracers = call(
        tracer_kernel,
        (tracer, tracer),
        scratch=((2, rows + 1, SUB, cols), (2, rows, SUB, cols)),
    )

    def strip_exchange(chosen):
        whole, half = partners(chosen)
        routes = [moves(chips_1)]
        routes += [moves((), at, turn) for turn in (whole, half) for at in (high, low)]
        routes += [moves(chips_2)] * bool(chips_2)

        def run(messages, inputs):
            return [send(m, pairs) for m, pairs in zip(messages, routes)], tracers(*inputs)

        return run

    received, (tracer_t, tracer_s) = lax.switch(
        choice,
        [strip_exchange(i) for i in branches],
        messages,
        (fields, flat, south, north, speed_n, speed_e, rises),
    )
    plane = real(rows, cols)
    out_u, out_v, out_sea, out_zonal, out_merid = call(
        functools.partial(wave_kernel, (rows, levels, lat_size)),
        (tracer, tracer, plane, plane, plane),
        scratch=((count, 2 * rows + 2 * MARGIN, width),),
        seam=True,
    )(seam, six, got_pair, *received[:5], base_u, base_v, *received[5:])
    return out_u, out_v, tracer_t, tracer_s, out_sea, out_zonal, out_merid


def solution(mesh):
    deep, plane = P(None, "lat", "lon"), P("lat", "lon")
    return jax.shard_map(
        functools.partial(on_device, mesh.shape["lon"], mesh.shape["lat"]),
        mesh=mesh,
        in_specs=(deep,) * 4 + (plane,) * 4 + (P("lon"),),
        out_specs=(deep,) * 4 + (plane,) * 3,
        check_vma=False,
    )
```

```python
import functools

import jax
import jax.numpy as jnp
from jax import lax
from jax.experimental import pallas as pl
from jax.experimental.pallas import tpu as pltpu
from jax.sharding import PartitionSpec as P

SUBSTEPS = 12
COURANT = 0.15
PRESSURE_GAIN = 0.1
CORIOLIS = 0.3
WAVE_MASS = 1.2
WAVE_MOMENTUM = 1.2
EPSILON = 1e-06

LANES = 128
SUB = 8
SLOT = 32
DEEP = 3
FIELDS = 4
MARGIN = 2 * SUBSTEPS
GRANT = 16 << 20


def lane_of(shape):
    return lax.broadcasted_iota(jnp.int32, shape, len(shape) - 1)


def wide_roll(values, offset):
    width = values.shape[-1]
    return pltpu.roll(values, (-offset) % width, values.ndim - 1)


def half_tiles(cols):
    assert cols == 2 * LANES
    return slice(0, LANES), slice(LANES, cols)


def own_slot(packed, k, first):
    return pltpu.roll(packed, lax.rem(first - SLOT * k + 2 * LANES, LANES), packed.ndim - 1)


def four_slots(parts, source_lane, lane):
    packed = None
    for k, part in enumerate(parts):
        moved = pltpu.roll(part, lax.rem(SLOT * k - source_lane + LANES, LANES), part.ndim - 1)
        packed = moved if packed is None else jnp.where(lane >= SLOT * k, moved, packed)
    return packed


def pack_kernel(u, v, t, s, sea, zonal, merid, tally, east, west):
    levels, rows, cols = u.shape
    lane = lane_of((SUB, LANES))
    lo, hi = half_tiles(cols)
    groups = rows // SUB
    for out, near, far, first in ((east, hi, lo, LANES - SLOT), (west, lo, hi, 0)):
        for g in range(groups):
            row = slice(SUB * g, SUB * (g + 1))
            for k in range(levels):
                parts = [q[k, row, near] for q in (u, v, t, s)]
                out[groups * k + g] = four_slots(parts, first, lane)
            parts = [q[row, near] for q in (sea, zonal, merid)]
            parts.append(tally[row, near].astype(jnp.float32))
            out[groups * levels + g] = four_slots(parts, first, lane)
        base, row = groups * (levels + 1), slice(rows - SUB, rows)
        edges = []
        for k, q in enumerate((u, v, t, s)):
            tile = jnp.swapaxes(q[:, row, near], 0, 1)
            for j in range(DEEP):
                out[base + k * DEEP + j] = tile[SUB - DEEP + j]
            edges.append(jnp.swapaxes(q[:, row, far], 0, 1))
        for j in range(DEEP):
            parts = [edge[SUB - DEEP + j] for edge in edges]
            out[base + FIELDS * DEEP + j] = four_slots(parts, first, lane)
        out[base + (FIELDS + 1) * DEEP] = tally[row, near].astype(jnp.float32)
        out[base + (FIELDS + 1) * DEEP + 1] = tally[row, far].astype(jnp.float32)


def halo_tile(from_east, from_west, k, lane):
    east = pltpu.roll(from_east, (-SLOT * k) % LANES, 1)
    west = pltpu.roll(from_west, (LANES - SLOT - SLOT * k) % LANES, 1)
    return jnp.where(lane < SLOT, east, jnp.where(lane >= LANES - SLOT, west, 0.0))


def widen_kernel(
    top_lat,
    seam,
    u,
    v,
    t,
    s,
    sea,
    zonal,
    merid,
    tally,
    from_west,
    from_east,
    fields,
    flat,
    msg_a,
    msg_b,
):
    levels, rows, cols = u.shape
    lane = lane_of((SUB, LANES))
    own, halo = slice(0, cols), slice(cols, cols + LANES)
    groups = rows // SUB
    for g in range(groups):
        row = slice(SUB * g, SUB * (g + 1))
        for k, q in enumerate((u, v, t, s)):
            fields[k, row, :, own] = jnp.swapaxes(q[:, row, :], 0, 1)
            tiles = [halo_tile(from_east[groups * i + g], from_west[groups * i + g], k, lane) for i in range(levels)]
            fields[k, row, :, halo] = jnp.swapaxes(jnp.stack(tiles), 0, 1)
        for k, q in enumerate((sea, zonal, merid, tally)):
            flat[k, row, own] = q[row, :].astype(jnp.float32)
            flat[k, row, halo] = halo_tile(from_east[groups * levels + g], from_west[groups * levels + g], k, lane)
    even = lax.rem(lax.axis_index("lat"), 2) == 0

    def fill(msg, first):
        for k in range(FIELDS):
            for q in range(DEEP):
                msg[k * DEEP + q] = fields[k, first + q]
        msg[FIELDS * DEEP, 0:DEEP, :] = flat[3, first : first + DEEP, :]
        msg[FIELDS * DEEP, DEEP:SUB, :] = jnp.zeros((SUB - DEEP, flat.shape[2]), jnp.float32)

    @pl.when(even)
    def _():
        fill(msg_a, rows - DEEP)
        fill(msg_b, 0)

    top = lax.axis_index("lat") == top_lat

    @pl.when(jnp.logical_not(even))
    def _():
        fill(msg_a, 0)

    @pl.when(jnp.logical_not(even) & jnp.logical_not(top))
    def _():
        fill(msg_b, rows - DEEP)

    @pl.when(top)
    def _():
        west, rest = fold_offset(seam, cols)
        first = jnp.where(west, LANES - SLOT, 0)
        base = groups * (levels + 1)
        tiles = [slice(LANES * i, LANES * (i + 1)) for i in range(cols // LANES + 1)]

        def beside(plane):
            return jnp.where(west, from_west[base + plane], from_east[base + plane])

        edges = [beside(FIELDS * DEEP + q) for q in range(DEEP)]
        for k in range(FIELDS):
            for q in range(DEEP):
                parts = [fields[k, rows - DEEP + q, :, at] for at in tiles]
                edge = own_slot(edges[q], k, first)
                line = facing_line(west, parts[:-1], parts[-1], beside(k * DEEP + q), edge)
                for at, ghost in zip(tiles, across_fold(line, rest, lane)):
                    msg_b[k * DEEP + DEEP - 1 - q, :, at] = -ghost if k < 2 else ghost
        half = (FIELDS + 1) * DEEP
        parts = [flat[3, rows - SUB : rows, at] for at in tiles]
        line = facing_line(west, parts[:-1], parts[-1], beside(half), beside(half + 1))
        for at, ghost in zip(tiles, across_fold(line, rest, lane)):
            msg_b[FIELDS * DEEP, :, at] = jnp.zeros_like(ghost)
            msg_b[FIELDS * DEEP, 0:1, at] = ghost[SUB - 1 : SUB, :]


def fold_offset(seam, cols):
    rest = lax.rem(seam[0], cols)
    return rest >= cols // 2, lax.rem(rest, LANES)


def across_fold(line, rest, lane):
    back = LANES - 1 - lane
    part = LANES - 1 - rest
    moved = [
        pltpu.roll(jnp.take_along_axis(x, back, axis=1), LANES - part, 1) for x in line[::-1]
    ]
    keep = lane < LANES - part
    out = [jnp.where(keep, p, q) for p, q in zip(moved, moved[1:])]
    last = jnp.where(lane < SLOT, out[-1], jnp.where(lane >= LANES - SLOT, out[0], 0.0))
    return out[1:-1] + [last]


def facing_line(west, whole, edge, half, half_edge):
    from_west = [half_edge, half] + whole + [edge]
    from_east = [edge] + whole + [half, half_edge]
    return [jnp.where(west, p, q) for p, q in zip(from_west, from_east)]


def weno_flux(speed, low2, low1, here, up1, up2, up3):
    ahead = speed >= 0.0
    a = jnp.where(ahead, low2, up3)
    b = jnp.where(ahead, low1, up2)
    c = jnp.where(ahead, here, up1)
    d = jnp.where(ahead, up1, here)
    e = jnp.where(ahead, up2, low1)
    g0, g1, g2, g3 = b - a, c - b, d - c, e - d
    third = 13.0 / 3.0

    def smooth(curve, slope):
        total = (4.0 * EPSILON + slope * slope) + third * (curve * curve)
        return total * total

    q0 = smooth(g1 - g0, 3.0 * g1 - g0)
    q1 = smooth(g2 - g1, g1 + g2)
    q2 = smooth(g3 - g2, g3 - 3.0 * g2)
    w0 = q1 * q2
    w1 = 6.0 * (q0 * q2)
    w2 = 3.0 * (q0 * q1)
    top = w0 * (5.0 * g1 - 2.0 * g0) + w1 * (g1 + 2.0 * g2) + w2 * (4.0 * g2 - g3)
    face = c + top / (6.0 * (w0 + w1 + w2))
    return COURANT * speed * face


def level_sums(values, level, upwards):
    for step in (1, 2, 4):
        moved = pltpu.roll(values, SUB - step if upwards else step, 0)
        inside = level < SUB - step if upwards else level >= step
        values = values + jnp.where(inside, moved, 0.0)
    return values


def row_of(k, j, at, rows, fields, south, north):
    if j < DEEP:
        return south[k * DEEP + j, :, at]
    if j < DEEP + rows:
        return fields[k, j - DEEP, :, at]
    return north[k * DEEP + j - DEEP - rows, :, at]


def north_fluxes(index, first, tiles, rows, fields, south, north, speed_n, flux_n):
    k, tile = lax.div(index, tiles), lax.rem(index, tiles)
    at = pl.ds(pl.multiple_of(tile * LANES, LANES), LANES)
    window = [row_of(first + k, j, at, rows, fields, south, north) for j in range(5)]
    for j in range(rows + 1):
        window.append(row_of(first + k, j + 5, at, rows, fields, south, north))
        flux_n[k, j, :, at] = weno_flux(speed_n[j, :, at], *window)
        window.pop(0)


def row_rate(q, speed, rise, north_step):
    flux = weno_flux(speed, *(wide_roll(q, i) if i else q for i in range(-2, 4)))
    vertical = rise * (q + pltpu.roll(q, 1, 0))
    below = pltpu.roll(vertical, SUB - 1, 0)
    return -(flux - wide_roll(flux, -1)) - north_step - (vertical - below)


def force_kernel(
    sizes,
    fields,
    flat,
    got_a,
    got_b,
    base_u,
    base_v,
    six,
    south,
    north,
    speed_n,
    speed_e,
    rises,
    wet,
    flux_n,
    press,
):
    rows, lat_size = sizes
    cols = base_u.shape[2]
    width = cols + LANES
    lat = lax.axis_index("lat")
    even = lax.rem(lat, 2) == 0
    planes = FIELDS * DEEP

    @pl.when(even)
    def _():
        south[...] = got_b[...]
        north[...] = got_a[...]

    @pl.when(jnp.logical_not(even))
    def _():
        south[...] = got_a[...]
        north[...] = got_b[...]

    @pl.when(lat == 0)
    def _():
        south[...] = jnp.zeros_like(south)

    level = lax.broadcasted_iota(jnp.int32, (SUB, width), 0)
    level_real = level.astype(jnp.float32)
    every = slice(None)

    def row(k, j):
        return row_of(k, j, every, rows, fields, south, north)

    def set_wet(index, tally_row):
        wet[index] = (level_real < jnp.broadcast_to(tally_row, (SUB, width))).astype(jnp.float32)

    set_wet(0, south[planes, DEEP - 1 : DEEP, :])
    for j in range(rows):
        set_wet(j + 1, flat[3, j : j + 1, :])
    set_wet(rows + 1, north[planes, 0:1, :])

    for j in range(rows + 1):
        speed_n[j] = 0.5 * (row(1, j + 2) + row(1, j + 3)) * wet[j] * wet[j + 1]
    for j in range(rows + 2):
        density = 0.8 * row(3, j + 2) - 0.2 * row(2, j + 2)
        press[j] = level_sums(density, level, False) - 0.5 * density

    tiles = width // LANES

    def northward(index, carry):
        north_fluxes(index, 0, tiles, rows, fields, south, north, speed_n, flux_n)
        return carry

    lax.fori_loop(0, 2 * tiles, northward, 0)
    total_rows = rows * lat_size

    def one_row(j, carry):
        mask = wet[j + 1]
        u, v = fields[0, j], fields[1, j]
        speed = 0.5 * (u + wide_roll(u, 1)) * mask * wide_roll(mask, 1)
        spread = speed - wide_roll(speed, -1) + (speed_n[j + 1] - speed_n[j])
        upward = -level_sums(spread, level, True)
        rise = jnp.where(level >= 1, (0.5 * COURANT) * upward, 0.0)
        speed_e[j] = speed
        rises[j] = rise
        rate_u = row_rate(u, speed, rise, flux_n[0, j + 1] - flux_n[0, j])
        rate_v = row_rate(v, speed, rise, flux_n[1, j + 1] - flux_n[1, j])
        place = (lat * rows + j).astype(jnp.float32)
        coriolis = CORIOLIS * (2.0 * (place + 0.5) / total_rows - 1.0)
        pressure = press[j + 1]
        grad_east = 0.5 * (wide_roll(pressure, 1) - wide_roll(pressure, -1))
        grad_north = 0.5 * (press[j + 2] - press[j])
        force_u = rate_u + coriolis * v - PRESSURE_GAIN * grad_east
        force_v = rate_v - coriolis * u - PRESSURE_GAIN * grad_north
        depth = jnp.maximum(flat[3, pl.ds(j, 1), :], 1.0)
        six[4, pl.ds(j, 1), :] = jnp.sum(mask * force_u, axis=0, keepdims=True) / depth
        six[5, pl.ds(j, 1), :] = jnp.sum(mask * force_v, axis=0, keepdims=True) / depth
        base_u[j] = (u + force_u)[:, :cols]
        base_v[j] = (v + force_v)[:, :cols]
        return carry

    lax.fori_loop(0, rows, one_row, 0)
    six[0:4] = flat[...]


def tracer_kernel(
    fields, flat, south, north, speed_n, speed_e, rises, tracer_t, tracer_s, flux_n, final
):
    rows = fields.shape[1]
    cols = tracer_t.shape[2]
    tiles = cols // LANES

    def northward(index, carry):
        north_fluxes(index, 2, tiles, rows, fields, south, north, speed_n, flux_n)
        return carry

    lax.fori_loop(0, 2 * tiles, northward, 0)
    level = lax.broadcasted_iota(jnp.int32, (SUB, cols), 0).astype(jnp.float32)
    aside = jnp.zeros((SUB, LANES), jnp.float32)

    def one_row(j, carry):
        tally = jnp.broadcast_to(flat[3, pl.ds(j, 1), pl.ds(0, cols)], (SUB, cols))
        mask = (level < tally).astype(jnp.float32)
        for k in (0, 1):
            q = fields[2 + k, j]
            step = jnp.concatenate([flux_n[k, j + 1] - flux_n[k, j], aside], axis=1)
            rate = row_rate(q, speed_e[j], rises[j], step)
            final[k, j] = mask * (q + rate)[:, :cols]
        return carry

    lax.fori_loop(0, rows, one_row, 0)
    for g in range(rows // SUB):
        row = slice(SUB * g, SUB * (g + 1))
        tracer_t[:, row, :] = jnp.swapaxes(final[0, row], 0, 1)
        tracer_s[:, row, :] = jnp.swapaxes(final[1, row], 0, 1)


def pair_kernel(sizes, seam, six, got_a, msg_1, full, full_low, half, half_low, *more):
    rows, lat_size = sizes
    cols = six.shape[2] - LANES
    lat = lax.axis_index("lat")
    even = lax.rem(lat, 2) == 0
    pair = lax.div(lat, 2)
    pair_even = lax.rem(pair, 2) == 0
    top = pair == lat_size // 2 - 1
    rest = MARGIN - rows
    lane = lane_of((SUB, LANES))

    def last(msg, lower, upper):
        msg[:, 0:rest, :] = lower[:, rows - rest : rows, :]
        msg[:, rest:MARGIN, :] = upper[...]

    def first(msg, lower, upper):
        msg[:, 0:rows, :] = lower[...]
        msg[:, rows:MARGIN, :] = upper[:, 0:rest, :]

    def across(lower, upper, low):
        whole_out, half_out = (full_low, half_low) if low else (full, half)
        west, _ = fold_offset(seam, cols)
        height = whole_out.shape[1]
        count = six.shape[0]
        for g in range(height // SUB):
            up = 2 * rows - height + SUB * g
            source, start = (lower, up) if up < rows else (upper, up - rows)
            row, out = slice(start, start + SUB), slice(SUB * g, SUB * (g + 1))
            edges, half_edges = [], []
            for k in range(count):
                left, right = (source[k, row, at] for at in half_tiles(cols))
                whole_out[2 * k, out, :] = left
                whole_out[2 * k + 1, out, :] = right
                half_out[k, out, :] = jnp.where(west, right, left)
                edges.append(source[k, row, cols:])
                half_edges.append(jnp.where(west, left, right))
            for i in range(0, count, 4):
                packed = four_slots(edges[i : i + 4], jnp.where(west, 0, LANES - SLOT), lane)
                whole_out[2 * count + i // 4, out, :] = packed
                packed = four_slots(half_edges[i : i + 4], jnp.where(west, LANES - SLOT, 0), lane)
                half_out[count + i // 4, out, :] = packed

    for bottom, lower, upper in ((True, six, got_a), (False, got_a, six)):
        mine = even if bottom else jnp.logical_not(even)

        @pl.when(mine & pair_even)
        def _(lower=lower, upper=upper):
            last(msg_1, lower, upper)
            if more:
                first(more[0], lower, upper)

        @pl.when(mine & jnp.logical_not(pair_even))
        def _(lower=lower, upper=upper):
            first(msg_1, lower, upper)
            if more:
                last(more[0], lower, upper)

        @pl.when(mine & top)
        def _(lower=lower, upper=upper, bottom=bottom):
            across(lower, upper, bottom)


def wave_kernel(
    sizes,
    seam,
    six,
    got_a,
    got_1,
    full,
    full_low,
    half,
    half_low,
    base_u,
    base_v,
    *rest,
):
    rows, levels, lat_size = sizes
    got_2 = rest[:-6]
    out_u, out_v, out_sea, out_zonal, out_merid, space = rest[-6:]
    cols = out_sea.shape[1]
    width = cols + LANES
    lat = lax.axis_index("lat")
    even = lax.rem(lat, 2) == 0
    pair = lax.div(lat, 2)
    pair_even = lax.rem(pair, 2) == 0
    top = pair == lat_size // 2 - 1
    lane = lane_of((SUB, LANES))
    own_low = slice(MARGIN, MARGIN + rows)
    own_high = slice(MARGIN + rows, MARGIN + 2 * rows)
    below, above = slice(0, MARGIN), slice(MARGIN + 2 * rows, 2 * MARGIN + 2 * rows)

    @pl.when(even)
    def _():
        space[:, own_low, :] = six[...]
        space[:, own_high, :] = got_a[...]

    @pl.when(jnp.logical_not(even))
    def _():
        space[:, own_low, :] = got_a[...]
        space[:, own_high, :] = six[...]

    @pl.when(pair_even)
    def _():
        space[:, below, :] = got_2[0][...] if got_2 else jnp.zeros_like(got_1)
        if got_2:

            @pl.when(pair == 0)
            def _():
                space[:, below, :] = jnp.zeros_like(got_1)

        space[:, above, :] = got_1[...]

    @pl.when(jnp.logical_not(pair_even))
    def _():
        space[:, below, :] = got_1[...]

    if got_2:

        @pl.when(jnp.logical_not(pair_even) & jnp.logical_not(top))
        def _():
            space[:, above, :] = got_2[0][...]

    def ghosts(whole, part):
        west, rest = fold_offset(seam, cols)
        turn = SUB - 1 - lax.broadcasted_iota(jnp.int32, (SUB, LANES), 0)
        count = six.shape[0]
        height = whole.shape[1]
        for k, parity in enumerate((1.0, -1.0, -1.0, 1.0, -1.0, -1.0)):
            for g in range(height // SUB):
                row = slice(SUB * g, SUB * (g + 1))
                edge = own_slot(whole[2 * count + k // 4, row, :], k % 4, jnp.where(west, 0, LANES - SLOT))
                half_edge = own_slot(part[count + k // 4, row, :], k % 4, jnp.where(west, LANES - SLOT, 0))
                tiles = [whole[2 * k, row, :], whole[2 * k + 1, row, :]]
                line = facing_line(west, tiles, edge, part[k, row, :], half_edge)
                place = above.start + height - SUB * (g + 1)
                for i, ghost in enumerate(across_fold(line, rest, lane)):
                    ghost = parity * jnp.take_along_axis(ghost, turn, axis=0)
                    space[k, place : place + SUB, LANES * i : LANES * (i + 1)] = ghost

    @pl.when(top & jnp.logical_not(even))
    def _():
        ghosts(full, half)

    @pl.when(top & even)
    def _():
        ghosts(full_low, half_low)

    height = rows + 2 * MARGIN
    window = pl.ds(pl.multiple_of(jnp.where(even, 0, rows), SUB), height)
    tally = space[3, window, :]
    wet = (tally > 0.0).astype(jnp.float32)
    thick = (0.5 * WAVE_MASS / levels) * tally
    total_rows = rows * lat_size
    place = lax.broadcasted_iota(jnp.int32, (height, width), 0) + (lat * rows - MARGIN)
    place = jnp.minimum(place, 2 * total_rows - 1 - place).astype(jnp.float32)
    turning = (CORIOLIS / SUBSTEPS) * (2.0 * (place + 0.5) / total_rows - 1.0)
    push_u = space[4, window, :] * (1.0 / SUBSTEPS)
    push_v = space[5, window, :] * (1.0 / SUBSTEPS)

    def step(index, state):
        sea, zonal, merid = state
        mass_e, mass_n = thick * zonal, thick * merid
        spread = (wide_roll(mass_e, 1) - wide_roll(mass_e, -1)) + (
            pltpu.roll(mass_n, height - 1, 0) - pltpu.roll(mass_n, 1, 0)
        )
        sea = wet * (sea - spread)
        slope_e = wide_roll(sea, 1) - wide_roll(sea, -1)
        slope_n = pltpu.roll(sea, height - 1, 0) - pltpu.roll(sea, 1, 0)
        half = 0.5 * WAVE_MOMENTUM
        next_zonal = wet * (zonal - half * slope_e + (turning * merid + push_u))
        next_merid = wet * (merid - half * slope_n + (push_v - turning * zonal))
        return sea, next_zonal, next_merid

    start = (space[0, window, :], space[1, window, :], space[2, window, :])
    sea, zonal, merid = lax.fori_loop(0, SUBSTEPS, step, start)
    mine = slice(MARGIN, MARGIN + rows)
    out_sea[...] = sea[mine, :cols]
    out_zonal[...] = zonal[mine, :cols]
    out_merid[...] = merid[mine, :cols]
    level = lax.broadcasted_iota(jnp.int32, (SUB, cols), 0).astype(jnp.float32)
    for base, flow, final, start_of, mean in (
        (base_u, out_u, out_zonal, 1, 4),
        (base_v, out_v, out_merid, 2, 5),
    ):
        for g in range(rows // SUB):
            block = []
            for j in range(SUB * g, SUB * (g + 1)):
                row = slice(j, j + 1)
                mask = level < jnp.broadcast_to(six[3, row, :cols], (SUB, cols))
                change = final[row, :] - six[start_of, row, :cols] - six[mean, row, :cols]
                block.append(mask.astype(jnp.float32) * (base[j] + jnp.broadcast_to(change, (SUB, cols))))
            flow[:, SUB * g : SUB * (g + 1), :] = jnp.swapaxes(jnp.stack(block), 0, 1)


def real(*shape):
    return jax.ShapeDtypeStruct(shape, jnp.float32)


def call(kernel, outs, scratch=(), seam=False, grant=GRANT):
    vmem = pl.BlockSpec(memory_space=pltpu.VMEM)

    def run(*args):
        specs = [vmem] * len(args)
        if seam:
            specs[0] = pl.BlockSpec(memory_space=pltpu.SMEM)
        return pl.pallas_call(
            kernel,
            out_shape=outs,
            in_specs=specs,
            out_specs=jax.tree.map(lambda _: vmem, outs),
            scratch_shapes=[pltpu.VMEM(shape, jnp.float32) for shape in scratch],
            compiler_params=pltpu.CompilerParams(vmem_limit_bytes=grant),
        )(*args)

    return run


def on_device(lon_size, lat_size, *arguments):
    u, v, t, s, sea, zonal, merid, tally, seam = arguments
    levels, rows, cols = u.shape
    width = cols + LANES
    assert levels == SUB and rows % SUB == 0 and lat_size % 4 == 0
    tile = lax.rem(lax.div(seam[0], cols) + lax.axis_index("lon"), lon_size)
    west_half = (lax.rem(seam[0], cols) >= cols // 2).astype(jnp.int32)
    choice = 2 * tile + west_half
    facing = lax.rem(tile + west_half + lon_size - 1, lon_size)

    def partners(chosen):
        turn, west = divmod(chosen, 2)
        return (turn, turn - 1) if west else (turn - 1, turn)

    def moves(lats, fold=(), turn=0):
        pairs = [(x * lat_size + a, x * lat_size + b) for a, b in lats for x in range(lon_size)]
        for a in fold:
            pairs += [(x * lat_size + a, (turn - x) % lon_size * lat_size + a) for x in range(lon_size)]
        busy = {a for a, _ in pairs}
        return pairs + [(i, i) for i in range(lon_size * lat_size) if i not in busy]

    def send(values, pairs):
        return lax.ppermute(values, ("lon", "lat"), pairs)

    def both(pairs):
        return [p for a, b in pairs for p in ((a, b), (b, a))]

    ring = [(i, (i + 1) % lon_size) for i in range(lon_size)]
    inside = both((a, a + 1) for a in range(0, lat_size, 2))
    between = both((a, a + 1) for a in range(1, lat_size - 1, 2))
    chips = lat_size // 2
    chips_1 = both((2 * c + b, 2 * c + 2 + b) for c in range(0, chips - 1, 2) for b in (0, 1))
    chips_2 = both((2 * c + b, 2 * c + 2 + b) for c in range(1, chips - 1, 2) for b in (0, 1))
    high, low = (lat_size - 1,), (lat_size - 2,)

    message = real((levels + 1) * rows // SUB + (FIELDS + 1) * DEEP + 2, SUB, LANES)
    flat_args = (u, v, t, s, sea, zonal, merid, tally)
    east, west = call(pack_kernel, (message, message), grant=None)(*flat_args)
    from_west = lax.ppermute(east, "lon", ring)
    from_east = lax.ppermute(west, "lon", [(b, a) for a, b in ring])

    deep = real(FIELDS * DEEP + 1, SUB, width)
    fields, flat, msg_a, msg_b = call(
        functools.partial(widen_kernel, lat_size - 1),
        (
            real(FIELDS, rows, SUB, width),
            real(FIELDS, rows, width),
            deep,
            deep,
        ),
        seam=True,
    )(seam, *flat_args, from_west, from_east)

    def deep_exchange(turn):
        def run(a, b):
            return send(a, moves(inside)), send(b, moves(between, high, turn))

        return run

    got_a, got_b = lax.switch(facing, [deep_exchange(i) for i in range(lon_size)], msg_a, msg_b)

    base = real(rows, SUB, cols)
    tracer = real(levels, rows, cols)
    wide = real(rows, SUB, width)
    base_u, base_v, six, south, north, speed_n, speed_e, rises = call(
        functools.partial(force_kernel, (rows, lat_size)),
        (base, base, real(6, rows, width), deep, deep, real(rows + 1, SUB, width), wide, wide),
        scratch=((rows + 2, SUB, width), (2, rows + 1, SUB, width), (rows + 2, SUB, width)),
    )(fields, flat, got_a, got_b)

    got_pair = send(six, moves(inside))
    count = six.shape[0]
    packs = -(-count // 4)
    strip = real(count, MARGIN, width)
    rest = MARGIN - rows
    strips = (strip,) + tuple(
        real(planes, height, LANES)
        for planes in (2 * count + packs, count + packs)
        for height in (MARGIN, rest)
    )
    strips += (strip,) * bool(chips_2)
    messages = call(functools.partial(pair_kernel, (rows, lat_size)), strips, seam=True)(
        seam, six, got_pair
    )
    tracers = call(
        tracer_kernel,
        (tracer, tracer),
        scratch=((2, rows + 1, SUB, cols), (2, rows, SUB, cols)),
    )

    def strip_exchange(chosen):
        whole, half = partners(chosen)
        routes = [moves(chips_1)]
        routes += [moves((), at, turn) for turn in (whole, half) for at in (high, low)]
        routes += [moves(chips_2)] * bool(chips_2)

        def run(messages, inputs):
            return [send(m, pairs) for m, pairs in zip(messages, routes)], tracers(*inputs)

        return run

    received, (tracer_t, tracer_s) = lax.switch(
        choice,
        [strip_exchange(i) for i in range(2 * lon_size)],
        messages,
        (fields, flat, south, north, speed_n, speed_e, rises),
    )
    plane = real(rows, cols)
    out_u, out_v, out_sea, out_zonal, out_merid = call(
        functools.partial(wave_kernel, (rows, levels, lat_size)),
        (tracer, tracer, plane, plane, plane),
        scratch=((count, 2 * rows + 2 * MARGIN, width),),
        seam=True,
    )(seam, six, got_pair, *received[:5], base_u, base_v, *received[5:])
    return out_u, out_v, tracer_t, tracer_s, out_sea, out_zonal, out_merid


def solution(mesh):
    deep, plane = P(None, "lat", "lon"), P("lat", "lon")
    return jax.shard_map(
        functools.partial(on_device, mesh.shape["lon"], mesh.shape["lat"]),
        mesh=mesh,
        in_specs=(deep,) * 4 + (plane,) * 4 + (P("lon"),),
        out_specs=(deep,) * 4 + (plane,) * 3,
        check_vma=False,
    )
```
